32 devices in a mesh: crop: 1, row: 32 (over z, y, x, core).
Axes of the slice: x: 2, y: 2, z: 4, core: 2. Of those that a mesh axis runs over, the one named last changes fastest.
Arguments:
- queries: bfloat16 [128, 128, 128], P(('crop', 'row')), may hold values from -4 to 4
- keys: bfloat16 [128, 128, 128], P(('crop', 'row')), may hold values from -4 to 4
- values: bfloat16 [128, 128, 128], P(('crop', 'row')), may hold values from -6 to 6
- grads_out: bfloat16 [128, 128, 128], P(('crop', 'row')), may hold values from -96 to 96
- log_norm: float32 [128, 4, 128], P(('crop', 'row')), may hold values from -90 to 102, as said below
- bias: bfloat16 [128, 4, 128], P(('crop', 'row')), may hold values from -4 to 4
Outputs:
- query_grad: bfloat16 [128, 128, 128], P(('crop', 'row'))
- key_grad: bfloat16 [128, 128, 128], P(('crop', 'row'))
- value_grad: bfloat16 [128, 128, 128], P(('crop', 'row'))
- bias_grad: float32 [128, 4, 128], P(('crop', 'row'))
The draws below stay inside these ranges and needn't reach their ends.
Inputs may be any that keep to these rules, and one draw needn't show every extreme that they name: log_norm[i, h, j] is the logarithm of the sum over k of exp(scores[i, h, j, k]), scores computed from the given queries, keys and bias.
All inputs are finite; a program needn't handle non-finite values.
Results may differ from the reference program's by a relative error of at most 0.0051.
Values may be sent and summed in bfloat16 or wider, within the bound.
No kernel may reach another device: no remote copies, remote signals or barrier semaphores. Data moves between devices by JAX's collectives and lax.ppermute only.
A program may use at most 64 MiB of HBM per device.

```python
import jax
import jax.numpy as jnp
from jax import lax

HEADS = 4
HEAD_DIM = 32
TOKENS = 128
CHANNELS = 128


def shared_fields(key):
    channels = HEADS * HEAD_DIM
    shape = (TOKENS, TOKENS, channels)
    query_field = jnp.clip(jax.random.normal(jax.random.fold_in(key, 101), shape, jnp.float32), -4.0, 4.0)
    key_field = jnp.clip(jax.random.normal(jax.random.fold_in(key, 103), shape, jnp.float32), -4.0, 4.0)
    bias_field = jnp.clip(jax.random.normal(jax.random.fold_in(key, 104), (TOKENS, HEADS, TOKENS), jnp.float32), -4.0, 4.0)
    return (query_field, key_field, bias_field)


def draw_queries(key, part):
    return shared_fields(key)[0].astype(jnp.bfloat16)


def draw_keys(key, part):
    return shared_fields(key)[1].astype(jnp.bfloat16)


def draw_bias(key, part):
    return shared_fields(key)[2].astype(jnp.bfloat16)


def draw_log_norm(key, part):
    query_field, key_field, bias_field = shared_fields(key)
    query_field = query_field.astype(jnp.bfloat16).astype(jnp.float32)
    key_field = key_field.astype(jnp.bfloat16).astype(jnp.float32)
    bias_heads = jnp.transpose(bias_field.astype(jnp.bfloat16).astype(jnp.float32), (1, 0, 2))
    score_scale = HEAD_DIM ** (-0.5)

    def one_row(inputs):
        query_row, key_row = inputs
        query_heads = query_row.reshape(TOKENS, HEADS, HEAD_DIM)
        key_heads = key_row.reshape(TOKENS, HEADS, HEAD_DIM)
        scores = jnp.einsum('jhd,khd->hjk', query_heads, key_heads) * score_scale + bias_heads
        return jax.scipy.special.logsumexp(scores, axis=-1)
    return lax.map(one_row, (query_field, key_field))


def raised(drawn, key, source, target, parts, factor):
    def block_of(dim):
        return (jnp.arange(drawn.shape[dim]) // (drawn.shape[dim] // parts)).reshape((-1,) + (1,) * (drawn.ndim - 1 - dim))

    near = jax.random.permutation(key, parts)[block_of(target)]
    far = (block_of(target) + parts // 2) % parts
    return jnp.where((block_of(source) == near) | (block_of(source) == far), factor * drawn, drawn)


def shard_levels(stream_key, shape, pieces, low, top_value):
    level, own = 1.0, jax.random.fold_in(stream_key, 6)
    for axis_at, blocks in pieces:
        draws = jnp.exp(jax.random.uniform(jax.random.fold_in(own, axis_at), (blocks,), jnp.float32, low / len(pieces), top_value / len(pieces)))
        level = level * jnp.repeat(draws, shape[axis_at] // blocks).reshape([-1 if axis == axis_at else 1 for axis in range(len(shape))])
    return level


def gaussian(key, dims, deviation, limit, cuts=(), held_as=jnp.bfloat16):
    array = deviation * jax.random.normal(key, dims, jnp.float32)
    if cuts:
        array = array * shard_levels(key, dims, cuts, -0.22, 0.18)
    return jnp.clip(array, -limit, limit).astype(held_as)


def noise_with(key, dims, deviation, limit, shards, heavy, dtype=jnp.bfloat16):
    result = deviation * jax.random.normal(key, dims, jnp.float32)
    if shards:
        result = result * shard_levels(key, dims, shards, -0.22, 0.18)
    return jnp.clip(raised(result, jax.random.fold_in(key, 3), *heavy), -limit, limit).astype(dtype)


def setup_inputs(seed: int = 0, part: int = 0) -> dict:
    seeds = jax.random.split(jax.random.key(seed), 7)
    own_keys = jax.random.split(jax.random.fold_in(seeds[6], part), 7)
    queries = draw_queries(jax.random.fold_in(jax.random.fold_in(seeds[6], part), 71), part)
    keys = draw_keys(jax.random.fold_in(jax.random.fold_in(seeds[6], part), 71), part)
    values = gaussian(own_keys[2], (TOKENS, TOKENS, CHANNELS), 1.0, 6.0, ((0, 32),))
    grads_out = noise_with(own_keys[3], (TOKENS, TOKENS, CHANNELS), 16.0, 96.0, ((0, 32),), (0, 1, 32, 2.75))
    log_norm = draw_log_norm(jax.random.fold_in(jax.random.fold_in(seeds[6], part), 71), part)
    bias = draw_bias(jax.random.fold_in(jax.random.fold_in(seeds[6], part), 71), part)
    return dict(queries=queries, keys=keys, values=values, grads_out=grads_out, log_norm=log_norm, bias=bias)


def reference(queries, keys, values, grads_out, log_norm, bias):
    length = queries.shape[1]
    head_count = bias.shape[1]
    pair_width = queries.shape[2]
    head_width = pair_width // head_count
    score_scale = head_width ** -0.5
    bias_heads = jnp.transpose(bias, (1, 0, 2)).astype(jnp.float32)

    def one_row(running, inputs):
        query_row, key_row, value_row, grad_row, norm_row = inputs
        query_heads = query_row.astype(jnp.float32).reshape(length, head_count, head_width)
        key_heads = key_row.astype(jnp.float32).reshape(length, head_count, head_width)
        value_heads = value_row.astype(jnp.float32).reshape(length, head_count, head_width)
        grad_heads = grad_row.astype(jnp.float32).reshape(length, head_count, head_width)
        scores = jnp.einsum("jhd,khd->hjk", query_heads, key_heads) * score_scale + bias_heads
        weights = jnp.exp(scores - norm_row[:, :, None])
        weight_grads = jnp.einsum("jhd,khd->hjk", grad_heads, value_heads)
        centre = jnp.sum(weights * weight_grads, axis=-1, keepdims=True)
        score_grads = weights * (weight_grads - centre)
        weights_low = lax.optimization_barrier(weights.astype(jnp.bfloat16)).astype(jnp.float32)
        grads_low = lax.optimization_barrier(score_grads.astype(jnp.bfloat16)).astype(jnp.float32)
        query_part = jnp.einsum("hjk,khd->jhd", grads_low, key_heads) * score_scale
        key_part = jnp.einsum("hjk,jhd->khd", grads_low, query_heads) * score_scale
        value_part = jnp.einsum("hjk,jhd->khd", weights_low, grad_heads)
        outputs = (query_part.reshape(length, pair_width).astype(jnp.bfloat16),
                   key_part.reshape(length, pair_width).astype(jnp.bfloat16),
                   value_part.reshape(length, pair_width).astype(jnp.bfloat16))
        return running + score_grads, outputs

    start_total = jnp.zeros((head_count, length, length), jnp.float32)
    total, grads = lax.scan(one_row, start_total, (queries, keys, values, grads_out, log_norm))
    return grads[0], grads[1], grads[2], jnp.transpose(total, (1, 0, 2))
```

```python
import jax
import jax.numpy as jnp
from jax import lax
from jax.sharding import PartitionSpec as P


def gather_rows(block, devices):
    copies = jnp.broadcast_to(block[None], (devices,) + block.shape)
    return lax.all_to_all(copies, "row", 0, 0)


def scatter_sum(partial, devices):
    rows = partial.shape[0] // devices
    parts = partial.astype(jnp.bfloat16).reshape((devices, rows) + partial.shape[1:])
    received = lax.all_to_all(parts, "row", 0, 0)
    return jnp.sum(received.astype(jnp.float32), axis=0)


def local(queries, keys, values, grads_out, log_norm, bias):
    head_count = bias.shape[1]
    local_rows, length, pair_width = queries.shape
    head_width = pair_width // head_count
    devices = lax.axis_size("row")
    score_scale = head_width ** (-0.5)
    gathered = gather_rows(bias, devices).reshape(length, head_count, length)

    def heads(array):
        return array.reshape(local_rows, length, head_count, head_width)

    def product(form, left, right):
        return jnp.einsum(form, left, right, preferred_element_type=jnp.float32)

    scores = product("rjhd,rkhd->rhjk", heads(queries), heads(keys)) * score_scale
    scores = scores + jnp.transpose(gathered, (1, 0, 2))[None].astype(jnp.float32)
    weights = jnp.exp(scores - log_norm[..., None])
    weight_grads = product("rjhd,rkhd->rhjk", heads(grads_out), heads(values))
    centre = jnp.sum(weights * weight_grads, axis=-1, keepdims=True)
    score_grads = weights * (weight_grads - centre)
    bias_part = jnp.transpose(jnp.sum(score_grads, axis=0), (1, 0, 2))
    bias_grad = scatter_sum(bias_part, devices)
    weights_low = weights.astype(jnp.bfloat16)
    grads_low = score_grads.astype(jnp.bfloat16)
    query_grad = product("rhjk,rkhd->rjhd", grads_low, heads(keys)) * score_scale
    key_grad = product("rhjk,rjhd->rkhd", grads_low, heads(queries)) * score_scale
    value_grad = product("rhjk,rjhd->rkhd", weights_low, heads(grads_out))

    def joined(array):
        return array.reshape(local_rows, length, pair_width).astype(jnp.bfloat16)

    return joined(query_grad), joined(key_grad), joined(value_grad), bias_grad


def solution(mesh):
    placed = P(("crop", "row"), None, None)
    return jax.shard_map(
        local, mesh=mesh, in_specs=(placed,) * 6, out_specs=(placed,) * 4, check_vma=False
    )
```

```python
import functools

import jax
import jax.numpy as jnp
from jax import lax
from jax.experimental import pallas as pl
from jax.experimental.pallas import tpu as pltpu
from jax.sharding import PartitionSpec as P

NT = (((1,), (1,)), ((), ()))
TN = (((0,), (0,)), ((), ()))
LANES = 128


def product(left, right, form):
    return lax.dot_general(left, right, form, preferred_element_type=jnp.float32)


def head_lanes(shape, head, width):
    lane = lax.broadcasted_iota(jnp.int32, shape, len(shape) - 1)
    return (lane >= head * width) & (lane < (head + 1) * width)


def only_head(array, head, width):
    return jnp.where(head_lanes(array.shape, head, width), array, jnp.zeros_like(array))


def before_kernel(heads, q_ref, k_ref, v_ref, g_ref, norm_ref, e_ref, f_ref, a_ref):
    rows, _, channels = q_ref.shape
    width = channels // heads
    scale = width ** (-0.5)
    norms = jnp.transpose(norm_ref[...])
    for head in range(heads):
        total = None
        for row in range(rows):
            column = row * heads + head
            scores = product(only_head(q_ref[row], head, width), k_ref[row], NT) * scale
            e = jnp.exp(scores - norms[:, column : column + 1])
            f = e * product(only_head(g_ref[row], head, width), v_ref[row], NT)
            e_ref[row, head] = e
            f_ref[row, head] = f
            total = f if total is None else total + f
        a_ref[head] = total


def bias_factor(bias_ref, spread_ref):
    devices, block, length = bias_ref.shape
    factor = jnp.exp(bias_ref[...].reshape(devices * block, length).astype(jnp.float32))
    for piece in range(length // LANES):
        spread_ref[piece] = factor[:, piece * LANES : (piece + 1) * LANES]


def factor_of(spread_ref, head, heads, length):
    here = pl.ds(head, length, stride=heads)
    pieces = [spread_ref[piece, here, :] for piece in range(length // LANES)]
    return pieces[0] if len(pieces) == 1 else jnp.concatenate(pieces, axis=1)


def middle_kernel(bias_ref, e_ref, f_ref, a_ref, part_ref, spread_ref, sums_ref):
    rows, heads, length, _ = e_ref.shape
    bias_factor(bias_ref, spread_ref)
    for head in range(heads):
        factor = factor_of(spread_ref, head, heads, length)
        total = a_ref[head]
        for row in range(rows):
            centre = jnp.sum(factor * f_ref[row, head], axis=1, keepdims=True)
            total = total - centre * e_ref[row, head]
        total = factor * total
        for piece in range(length // LANES):
            lanes = total[:, piece * LANES : (piece + 1) * LANES]
            sums_ref[piece, pl.ds(head, length, stride=heads), :] = lanes
    for piece in range(length // LANES):
        lanes = sums_ref[piece].astype(jnp.bfloat16).reshape(part_ref.shape[:2] + (LANES,))
        part_ref[:, :, piece * LANES : (piece + 1) * LANES] = lanes


def after_kernel(
    bias_ref, e_ref, f_ref, q_ref, k_ref, g_ref, dq_ref, dk_ref, dv_ref, spread_ref, w_ref, s_ref
):
    rows, heads, length, _ = e_ref.shape
    width = q_ref.shape[2] // heads
    scale = width ** (-0.5)
    bias_factor(bias_ref, spread_ref)
    for row in range(rows):
        for head in range(heads):
            factor = factor_of(spread_ref, head, heads, length)
            e, f = e_ref[row, head], f_ref[row, head]
            centre = jnp.sum(factor * f, axis=1, keepdims=True)
            here = pl.ds(head * length, length)
            w_ref[here, :] = (factor * e).astype(jnp.bfloat16)
            s_ref[here, :] = (factor * (f - centre * e)).astype(jnp.bfloat16)
        grads = s_ref[...]
        total = None
        for head in range(heads):
            term = product(
                grads[head * length : (head + 1) * length],
                only_head(k_ref[row], head, width),
                (((1,), (0,)), ((), ())),
            )
            total = term if total is None else total + term
        dq_ref[row] = (total * scale).astype(jnp.bfloat16)
        stacked = jnp.concatenate([only_head(q_ref[row], h, width) for h in range(heads)], 0)
        dk_ref[row] = (product(grads, stacked, TN) * scale).astype(jnp.bfloat16)
        stacked = jnp.concatenate([only_head(g_ref[row], h, width) for h in range(heads)], 0)
        dv_ref[row] = product(w_ref[...], stacked, TN).astype(jnp.bfloat16)


def call(kernel, name, outputs, scratch=(), flops=0, limit=16 << 20):
    return pl.pallas_call(
        kernel,
        name=name,
        out_shape=outputs,
        scratch_shapes=scratch,
        compiler_params=pltpu.CompilerParams(vmem_limit_bytes=limit),
        cost_estimate=pl.CostEstimate(flops=flops, bytes_accessed=1 << 20, transcendentals=0),
    )


def local(queries, keys, values, grads_out, log_norm, bias):
    heads = bias.shape[1]
    rows, length, channels = queries.shape
    devices = lax.axis_size("row")
    shape, f32, bf16 = jax.ShapeDtypeStruct, jnp.float32, jnp.bfloat16
    block = (rows * heads, length)
    tiles = (rows, heads, length, length)
    copies = jnp.broadcast_to(bias.reshape(block)[None], (devices,) + block)
    gathered = lax.all_to_all(copies, "row", 0, 0)
    e, f, a = call(
        functools.partial(before_kernel, heads),
        "before",
        (shape(tiles, f32), shape(tiles, f32), shape(tiles[1:], f32)),
        flops=1 << 30,
    )(queries, keys, values, grads_out, log_norm.reshape(block))
    wide = pltpu.VMEM((length // LANES, length * heads, LANES), f32)
    part = call(
        middle_kernel, "middle", shape((devices,) + block, bf16), (wide, wide), flops=1 << 20
    )(gathered, e, f, a)
    received = lax.all_to_all(part, "row", 0, 0)
    narrow = pltpu.VMEM((length * heads, length), bf16)
    grads = call(
        after_kernel,
        "after",
        (shape(queries.shape, bf16),) * 3,
        (wide, narrow, narrow),
        flops=1 << 30,
    )(gathered, e, f, queries, keys, grads_out)
    bias_grad = jnp.sum(received.astype(f32), axis=0).reshape(bias.shape)
    return (*grads, bias_grad)


def solution(mesh):
    placed = P(("crop", "row"), None, None)
    return jax.shard_map(
        local, mesh=mesh, in_specs=(placed,) * 6, out_specs=(placed,) * 4, check_vma=False
    )
```

```python
import functools
import math

import jax
import jax.numpy as jnp
from jax import lax
from jax.experimental import pallas as pl
from jax.experimental.pallas import tpu as pltpu
from jax.sharding import PartitionSpec as P

NN = (((1,), (0,)), ((), ()))
NT = (((1,), (1,)), ((), ()))
LANES = 128
LOG2E = math.log2(math.e)


def product(left, right, form=NN):
    return lax.dot_general(left, right, form, preferred_element_type=jnp.float32)


def head_lanes(shape, head, width):
    lane = lax.broadcasted_iota(jnp.int32, shape, len(shape) - 1)
    return (lane >= head * width) & (lane < (head + 1) * width)


def only_head(array, head, width):
    return jnp.where(head_lanes(array.shape, head, width), array, jnp.zeros_like(array))


def spread_rows(spread_ref, array):
    for piece in range(array.shape[1] // LANES):
        spread_ref[piece] = array[:, piece * LANES : (piece + 1) * LANES]


def head_rows(spread_ref, head, heads, length):
    here = pl.ds(head, length, stride=heads)
    pieces = [spread_ref[piece, here, :] for piece in range(spread_ref.shape[0])]
    return pieces[0] if len(pieces) == 1 else jnp.concatenate(pieces, axis=1)


def keep_head_rows(spread_ref, head, heads, array):
    length = array.shape[0]
    for piece in range(spread_ref.shape[0]):
        lanes = array[:, piece * LANES : (piece + 1) * LANES]
        spread_ref[piece, pl.ds(head, length, stride=heads), :] = lanes


def load_kernel(bias_hbm, norm_hbm, g_hbm, copies_ref, norm_ref, g_ref, bias_ref, sems):
    pairs = ((bias_hbm, bias_ref), (norm_hbm, norm_ref), (g_hbm, g_ref))
    moves = [pltpu.make_async_copy(a, b, sems.at[n]) for n, (a, b) in enumerate(pairs)]
    for move in moves:
        move.start()
    moves[0].wait()
    copies_ref[...] = jnp.broadcast_to(bias_ref[...][None], copies_ref.shape)
    for move in moves[1:]:
        move.wait()


def store_kernel(
    received_ref, dq_ref, dk_ref, dv_ref, sum_hbm, dq_hbm, dk_hbm, dv_hbm, sum_ref, sems
):
    pairs = ((dq_ref, dq_hbm), (dk_ref, dk_hbm), (dv_ref, dv_hbm), (sum_ref, sum_hbm))
    moves = [pltpu.make_async_copy(a, b, sems.at[n]) for n, (a, b) in enumerate(pairs)]
    for move in moves[:3]:
        move.start()
    sum_ref[...] = jnp.sum(received_ref[...].astype(jnp.float32), axis=0)
    moves[3].start()
    for move in moves:
        move.wait()


def attend_kernel(
    heads, bias_ref, q_ref, k_ref, v_ref, g_ref, norm_ref,
    part_ref, dq_ref, dk_ref, dv_ref, spread_ref,
):
    rows, length, channels = q_ref.shape
    width = channels // heads
    scale = width ** (-0.5)
    low = jnp.bfloat16
    every = range(heads)
    bias = bias_ref[...].reshape(heads * length, length).astype(jnp.float32) * LOG2E
    spread_rows(spread_ref, bias)
    logits = [head_rows(spread_ref, head, heads, length) for head in every]
    norms = jnp.transpose(norm_ref[...]) * LOG2E

    def stack(array):
        return jnp.concatenate([only_head(array, head, width) for head in every], 0)

    def turned_stack(array):
        turned = jnp.transpose(array)
        line = lax.broadcasted_iota(jnp.int32, turned.shape, 0)
        zero = jnp.zeros_like(turned)
        kept = [(line >= h * width) & (line < (h + 1) * width) for h in every]
        return jnp.concatenate([jnp.where(mask, turned, zero) for mask in kept], 1)

    sums = [None] * heads
    for row in range(rows):
        q, k, v, g = q_ref[row], k_ref[row], v_ref[row], g_ref[row]
        s_all, p_all = product(stack(q), k, NT), product(stack(g), v, NT)
        w_low, s_low = [], []
        for head in every:
            column = row * heads + head
            weights = jnp.exp2(
                s_all[head * length : (head + 1) * length] * (scale * LOG2E) + (logits[head] - norms[:, column : column + 1])
            )
            slopes = p_all[head * length : (head + 1) * length]
            centre = jnp.sum(weights * slopes, axis=1, keepdims=True)
            grads = weights * (slopes - centre)
            sums[head] = grads if row == 0 else sums[head] + grads
            w_low.append(weights.astype(low))
            s_low.append(grads.astype(low))
        dq = product(jnp.concatenate(s_low, 1), stack(k))
        dkt = product(turned_stack(q), jnp.concatenate(s_low, 0))
        dvt = product(turned_stack(g), jnp.concatenate(w_low, 0))
        dq_ref[row] = (dq * scale).astype(low)
        dk_ref[row] = jnp.transpose((dkt * scale).astype(low))
        dv_ref[row] = jnp.transpose(dvt.astype(low))
    for head in every:
        keep_head_rows(spread_ref, head, heads, sums[head])
    for piece in range(length // LANES):
        lanes = spread_ref[piece].astype(low).reshape(part_ref.shape[:2] + (LANES,))
        part_ref[:, :, piece * LANES : (piece + 1) * LANES] = lanes


def call(kernel, name, outputs, scratch=(), ins=None, outs=None):
    def place(space):
        return pl.BlockSpec(memory_space=space)

    specs = {}
    if ins is not None:
        specs["in_specs"] = [place(space) for space in ins]
    if outs is not None:
        specs["out_specs"] = tuple(place(space) for space in outs)
    return pl.pallas_call(
        kernel,
        name=name,
        out_shape=outputs,
        scratch_shapes=scratch,
        compiler_params=pltpu.CompilerParams(vmem_limit_bytes=24 << 20),
        **specs,
    )


def local(queries, keys, values, grads_out, log_norm, bias):
    heads = bias.shape[1]
    rows, length, channels = queries.shape
    devices = lax.axis_size("row")
    shape, f32, bf16 = jax.ShapeDtypeStruct, jnp.float32, jnp.bfloat16
    hbm, vmem, dma = pltpu.HBM, pltpu.VMEM, pltpu.SemaphoreType.DMA
    block = (rows * heads, length)
    exchanged = shape((devices,) + block, bf16)
    pair = shape(queries.shape, bf16)
    copies, norms, cotangents = call(
        load_kernel,
        "load",
        (exchanged, shape(block, f32), pair),
        (vmem(block, bf16), dma((3,))),
        (hbm,) * 3,
        (vmem,) * 3,
    )(*(pltpu.with_memory_space_constraint(array, hbm) for array in (bias.reshape(block), log_norm.reshape(block), grads_out)))
    gathered = lax.all_to_all(copies, "row", 0, 0)
    wide = vmem((length // LANES, length * heads, LANES), f32)
    part, *grads = call(
        functools.partial(attend_kernel, heads), "attend", (exchanged,) + (pair,) * 3, (wide,)
    )(gathered, queries, keys, values, cotangents, norms)
    received = lax.all_to_all(part, "row", 0, 0)
    bias_grad, *grads = call(
        store_kernel,
        "store",
        (shape(block, f32),) + (pair,) * 3,
        (vmem(block, f32), dma((4,))),
        (vmem,) * 4,
        (hbm,) * 4,
    )(received, *grads)
    return (*grads, bias_grad.reshape(bias.shape))


def solution(mesh):
    placed = P(("crop", "row"), None, None)
    return jax.shard_map(
        local, mesh=mesh, in_specs=(placed,) * 6, out_specs=(placed,) * 4, check_vma=False
    )
```

```python
import functools

import jax
import jax.numpy as jnp
from jax import lax
from jax.experimental import pallas as pl
from jax.experimental.pallas import tpu as pltpu
from jax.sharding import PartitionSpec as P

NN = (((1,), (0,)), ((), ()))
NT = (((1,), (1,)), ((), ()))
LANES = 128


def product(left, right, form=NN):
    return lax.dot_general(left, right, form, preferred_element_type=jnp.float32)


def head_lanes(shape, head, width):
    lane = lax.broadcasted_iota(jnp.int32, shape, len(shape) - 1)
    return (lane >= head * width) & (lane < (head + 1) * width)


def only_head(array, head, width):
    return jnp.where(head_lanes(array.shape, head, width), array, jnp.zeros_like(array))


def spread_rows(spread_ref, array):
    for piece in range(array.shape[1] // LANES):
        spread_ref[piece] = array[:, piece * LANES : (piece + 1) * LANES]


def head_rows(spread_ref, head, heads, length):
    here = pl.ds(head, length, stride=heads)
    pieces = [spread_ref[piece, here, :] for piece in range(spread_ref.shape[0])]
    return pieces[0] if len(pieces) == 1 else jnp.concatenate(pieces, axis=1)


def keep_head_rows(spread_ref, head, heads, array):
    length = array.shape[0]
    for piece in range(spread_ref.shape[0]):
        lanes = array[:, piece * LANES : (piece + 1) * LANES]
        spread_ref[piece, pl.ds(head, length, stride=heads), :] = lanes


def load_kernel(bias_hbm, norm_hbm, g_hbm, copies_ref, norm_ref, g_ref, bias_ref, sems):
    pairs = [(bias_hbm, bias_ref), (norm_hbm, norm_ref)]
    pairs += [(g_hbm.at[row], g_ref.at[row]) for row in range(g_ref.shape[0])]
    moves = [pltpu.make_async_copy(a, b, sems.at[n]) for n, (a, b) in enumerate(pairs)]
    for move in moves:
        move.start()
    moves[0].wait()
    copies_ref[...] = jnp.broadcast_to(bias_ref[...][None], copies_ref.shape)
    for move in moves[1:]:
        move.wait()


def store_kernel(
    received_ref, dq_ref, dk_ref, dv_ref, sum_hbm, dq_hbm, dk_hbm, dv_hbm, sum_ref, sems
):
    pairs = ((dq_ref, dq_hbm), (dk_ref, dk_hbm), (dv_ref, dv_hbm), (sum_ref, sum_hbm))
    moves = [pltpu.make_async_copy(a, b, sems.at[n]) for n, (a, b) in enumerate(pairs)]
    for move in moves[:3]:
        move.start()
    sum_ref[...] = jnp.sum(received_ref[...].astype(jnp.float32), axis=0)
    moves[3].start()
    for move in moves:
        move.wait()


def identity(length, dtype):
    rows = lax.broadcasted_iota(jnp.int32, (length, length), 0)
    columns = lax.broadcasted_iota(jnp.int32, (length, length), 1)
    return jnp.where(rows == columns, 1.0, 0.0).astype(dtype)


def joined(parts, width):
    total = parts[0]
    for head in range(1, len(parts)):
        total = jnp.where(head_lanes(total.shape, head, width), parts[head], total)
    return total

def attend_kernel(
    heads, bias_ref, q_ref, k_ref, v_ref, g_ref, norm_ref,
    part_ref, dq_ref, dk_ref, dv_ref, spread_ref,
):
    rows, length, channels = q_ref.shape
    width = channels // heads
    scale = width ** (-0.5)
    low = jnp.bfloat16
    every = range(heads)
    eye = identity(length, low)

    def stack(array):
        return jnp.concatenate([only_head(array, head, width) for head in every], 0)

    def cut(array, head):
        return array[head * length : (head + 1) * length]

    def mine(array, head):
        return array[head * width : (head + 1) * width]

    spread_rows(spread_ref, bias_ref[...].reshape(heads * length, length).astype(jnp.float32))
    rows_of = [head_rows(spread_ref, head, heads, length).astype(low) for head in every]
    logits = [product(eye, rows_of[head], NT) for head in every]
    norms = norm_ref[...]
    sums = [None] * heads

    def scored(row):
        return (
            product(stack(k_ref[row]), q_ref[row], NT),
            product(stack(v_ref[row]), g_ref[row], NT),
        )

    ahead = scored(0)
    for row in range(rows):
        q, k, v, g = q_ref[row], k_ref[row], v_ref[row], g_ref[row]
        s_all, p_all = ahead
        if row + 1 < rows:
            ahead = scored(row + 1)
        kt = jnp.transpose(k)
        w_low, s_low = [], []
        for head in every:
            line = row * heads + head
            weights = jnp.exp(
                cut(s_all, head) * scale + (logits[head] - norms[line : line + 1])
            )
            slopes = cut(p_all, head)
            centre = jnp.sum(weights * slopes, axis=0, keepdims=True)
            grads = weights * (slopes - centre)
            sums[head] = grads if row == 0 else sums[head] + grads
            if row == rows - 1:
                upright = jnp.transpose(sums[head].astype(low)).astype(jnp.float32)
                keep_head_rows(spread_ref, head, heads, upright)
            w_low.append(weights.astype(low))
            s_low.append(grads.astype(low))
        dk = product(jnp.concatenate(s_low, 0), q)
        dv = product(jnp.concatenate(w_low, 0), g)
        dqt = jnp.concatenate([product(mine(kt, h), s_low[h]) for h in every], 0)
        dk_ref[row] = (joined([cut(dk, h) for h in every], width) * scale).astype(low)
        dv_ref[row] = joined([cut(dv, h) for h in every], width).astype(low)
        dq_ref[row] = jnp.transpose((dqt * scale).astype(low))
    for piece in range(length // LANES):
        lanes = spread_ref[piece].astype(low).reshape(part_ref.shape[:2] + (LANES,))
        part_ref[:, :, piece * LANES : (piece + 1) * LANES] = lanes


def call(kernel, name, outputs, scratch=(), ins=None, outs=None):
    def place(space):
        return pl.BlockSpec(memory_space=space)

    specs = {}
    if ins is not None:
        specs["in_specs"] = [place(space) for space in ins]
    if outs is not None:
        specs["out_specs"] = tuple(place(space) for space in outs)
    return pl.pallas_call(
        kernel,
        name=name,
        out_shape=outputs,
        scratch_shapes=scratch,
        compiler_params=pltpu.CompilerParams(vmem_limit_bytes=24 << 20),
        **specs,
    )


def local(queries, keys, values, grads_out, log_norm, bias):
    heads = bias.shape[1]
    rows, length, channels = queries.shape
    devices = lax.axis_size("row")
    shape, f32, bf16 = jax.ShapeDtypeStruct, jnp.float32, jnp.bfloat16
    held = pltpu.with_memory_space_constraint
    hbm, vmem, dma = pltpu.HBM, pltpu.VMEM, pltpu.SemaphoreType.DMA
    block = (rows * heads, length)
    exchanged = shape((devices,) + block, bf16)
    pair = shape(queries.shape, bf16)
    copies, norms, cotangents = call(
        load_kernel,
        "load",
        (exchanged, shape(block, f32), pair),
        (vmem(block, bf16), dma((2 + rows,))),
        (hbm,) * 3,
        (vmem,) * 3,
    )(*(held(array, hbm) for array in (bias.reshape(block), log_norm.reshape(block), grads_out)))
    gathered = lax.all_to_all(copies, "row", 0, 0)
    wide = vmem((length // LANES, length * heads, LANES), f32)
    part, *grads = call(
        functools.partial(attend_kernel, heads), "attend", (exchanged,) + (pair,) * 3, (wide,)
    )(gathered, queries, keys, values, cotangents, norms)
    received = lax.all_to_all(part, "row", 0, 0)
    bias_grad, *grads = call(
        store_kernel,
        "store",
        (shape(block, f32),) + (pair,) * 3,
        (vmem(block, f32), dma((4,))),
        (vmem,) * 4,
        (hbm,) * 4,
    )(received, *grads)
    return (*grads, bias_grad.reshape(bias.shape))


def solution(mesh):
    placed = P(("crop", "row"), None, None)
    return jax.shard_map(
        local, mesh=mesh, in_specs=(placed,) * 6, out_specs=(placed,) * 4, check_vma=False
    )
```

```python
import functools

import jax
import jax.numpy as jnp
from jax import lax
from jax.experimental import pallas as pl
from jax.experimental.pallas import tpu as pltpu
from jax.sharding import PartitionSpec as P

NN = (((1,), (0,)), ((), ()))
NT = (((1,), (1,)), ((), ()))
LANES = 128


def product(left, right, form=NN):
    return lax.dot_general(left, right, form, preferred_element_type=jnp.float32)


def head_lanes(shape, head, width):
    lane = lax.broadcasted_iota(jnp.int32, shape, len(shape) - 1)
    return (lane >= head * width) & (lane < (head + 1) * width)


def only_head(array, head, width):
    return jnp.where(head_lanes(array.shape, head, width), array, jnp.zeros_like(array))


def spread_rows(spread_ref, array):
    for piece in range(array.shape[1] // LANES):
        spread_ref[piece] = array[:, piece * LANES : (piece + 1) * LANES]


def head_rows(spread_ref, head, heads, length):
    here = pl.ds(head, length, stride=heads)
    pieces = [spread_ref[piece, here, :] for piece in range(spread_ref.shape[0])]
    return pieces[0] if len(pieces) == 1 else jnp.concatenate(pieces, axis=1)


def keep_head_rows(spread_ref, head, heads, array):
    length = array.shape[0]
    for piece in range(spread_ref.shape[0]):
        lanes = array[:, piece * LANES : (piece + 1) * LANES]
        spread_ref[piece, pl.ds(head, length, stride=heads), :] = lanes


def load_kernel(bias_ref, copies_ref):
    copies_ref[...] = jnp.broadcast_to(bias_ref[...][None], copies_ref.shape)


def store_kernel(
    received_ref, dq_ref, dk_ref, dv_ref, sum_hbm, dq_hbm, dk_hbm, dv_hbm, sum_ref, sems
):
    pairs = ((dq_ref, dq_hbm), (dk_ref, dk_hbm), (dv_ref, dv_hbm), (sum_ref, sum_hbm))
    moves = [pltpu.make_async_copy(a, b, sems.at[n]) for n, (a, b) in enumerate(pairs)]
    for move in moves[:3]:
        move.start()
    sum_ref[...] = jnp.sum(received_ref[...].astype(jnp.float32), axis=0)
    moves[3].start()
    for move in moves:
        move.wait()


def identity(length, dtype):
    rows = lax.broadcasted_iota(jnp.int32, (length, length), 0)
    columns = lax.broadcasted_iota(jnp.int32, (length, length), 1)
    return jnp.where(rows == columns, 1.0, 0.0).astype(dtype)


def joined(parts, width):
    total = parts[0]
    for head in range(1, len(parts)):
        total = jnp.where(head_lanes(total.shape, head, width), parts[head], total)
    return total

def attend_kernel(
    heads, bias_ref, q_ref, k_ref, v_ref, g_ref, norm_ref,
    part_ref, dq_ref, dk_ref, dv_ref, spread_ref,
):
    rows, length, channels = q_ref.shape
    width = channels // heads
    scale = width ** (-0.5)
    low = jnp.bfloat16
    every = range(heads)
    eye = identity(length, low)

    def stack(array):
        return jnp.concatenate([only_head(array, head, width) for head in every], 0)

    def cut(array, head):
        return array[head * length : (head + 1) * length]

    def mine(array, head):
        return array[head * width : (head + 1) * width]

    spread_rows(spread_ref, bias_ref[...].reshape(heads * length, length).astype(jnp.float32))
    rows_of = [head_rows(spread_ref, head, heads, length).astype(low) for head in every]
    turned = product(eye, jnp.concatenate(rows_of, 0), NT)
    logits = [turned[:, head * length : (head + 1) * length] for head in every]
    norms = norm_ref[...]
    sums = [None] * heads

    def scored(row):
        return (
            product(stack(k_ref[row]), q_ref[row], NT),
            product(stack(v_ref[row]), g_ref[row], NT),
        )

    ahead = scored(0)
    for row in range(rows):
        q, k, v, g = q_ref[row], k_ref[row], v_ref[row], g_ref[row]
        s_all, p_all = ahead
        if row + 1 < rows:
            ahead = scored(row + 1)
        kt = jnp.transpose(k)
        w_low, s_low = [], []
        for head in every:
            line = row * heads + head
            weights = jnp.exp(
                cut(s_all, head) * scale + (logits[head] - norms[line : line + 1])
            )
            slopes = cut(p_all, head)
            centre = jnp.sum(weights * slopes, axis=0, keepdims=True)
            grads = weights * (slopes - centre)
            sums[head] = grads if row == 0 else sums[head] + grads
            if row == rows - 1:
                upright = jnp.transpose(sums[head].astype(low)).astype(jnp.float32)
                keep_head_rows(spread_ref, head, heads, upright)
            w_low.append(weights.astype(low))
            s_low.append(grads.astype(low))
        dk = product(jnp.concatenate(s_low, 0), q)
        dv = product(jnp.concatenate(w_low, 0), g)
        dqt = jnp.concatenate([product(mine(kt, h), s_low[h]) for h in every], 0)
        dk_ref[row] = (joined([cut(dk, h) for h in every], width) * scale).astype(low)
        dv_ref[row] = joined([cut(dv, h) for h in every], width).astype(low)
        dq_ref[row] = jnp.transpose((dqt * scale).astype(low))
    for piece in range(length // LANES):
        lanes = spread_ref[piece].astype(low).reshape(part_ref.shape[:2] + (LANES,))
        part_ref[:, :, piece * LANES : (piece + 1) * LANES] = lanes


def call(kernel, name, outputs, scratch=(), ins=None, outs=None, cost=None):
    def place(space):
        return pl.BlockSpec(memory_space=space)

    specs = {}
    if ins is not None:
        specs["in_specs"] = [place(space) for space in ins]
    if outs is not None:
        specs["out_specs"] = tuple(place(space) for space in outs)
    return pl.pallas_call(
        kernel,
        name=name,
        cost_estimate=cost,
        out_shape=outputs,
        scratch_shapes=scratch,
        compiler_params=pltpu.CompilerParams(vmem_limit_bytes=24 << 20),
        **specs,
    )


def local(queries, keys, values, grads_out, log_norm, bias):
    heads = bias.shape[1]
    rows, length, channels = queries.shape
    devices = lax.axis_size("row")
    shape, f32, bf16 = jax.ShapeDtypeStruct, jnp.float32, jnp.bfloat16
    held = pltpu.with_memory_space_constraint
    hbm, vmem, dma = pltpu.HBM, pltpu.VMEM, pltpu.SemaphoreType.DMA
    block = (rows * heads, length)
    exchanged = shape((devices,) + block, bf16)
    pair = shape(queries.shape, bf16)
    copies = call(load_kernel, "load", exchanged, cost=pl.CostEstimate(flops=1 << 34, bytes_accessed=1 << 26, transcendentals=0))(bias.reshape(block))
    gathered = lax.all_to_all(copies, "row", 0, 0)
    wide = vmem((length // LANES, length * heads, LANES), f32)
    part, *grads = call(
        functools.partial(attend_kernel, heads), "attend", (exchanged,) + (pair,) * 3, (wide,)
    )(gathered, queries, keys, values, grads_out, log_norm.reshape(block))
    received = lax.all_to_all(part, "row", 0, 0)
    bias_grad, *grads = call(
        store_kernel,
        "store",
        (shape(block, f32),) + (pair,) * 3,
        (vmem(block, f32), dma((4,))),
        (vmem,) * 4,
        (hbm,) * 4,
    )(received, *grads)
    return (*grads, bias_grad.reshape(bias.shape))


def solution(mesh):
    placed = P(("crop", "row"), None, None)
    return jax.shard_map(
        local, mesh=mesh, in_specs=(placed,) * 6, out_specs=(placed,) * 4, check_vma=False
    )
```

```python
import functools

import jax
import jax.numpy as jnp
from jax import lax
from jax.experimental import pallas as pl
from jax.experimental.pallas import tpu as pltpu
from jax.sharding import PartitionSpec as P

NN = (((1,), (0,)), ((), ()))
NT = (((1,), (1,)), ((), ()))
LANES = 128


def product(left, right, form=NN):
    return lax.dot_general(left, right, form, preferred_element_type=jnp.float32)


def head_lanes(shape, head, width):
    lane = lax.broadcasted_iota(jnp.int32, shape, len(shape) - 1)
    return (lane >= head * width) & (lane < (head + 1) * width)


def only_head(array, head, width):
    return jnp.where(head_lanes(array.shape, head, width), array, jnp.zeros_like(array))


def spread_rows(spread_ref, array):
    for piece in range(array.shape[1] // LANES):
        spread_ref[piece] = array[:, piece * LANES : (piece + 1) * LANES]


def head_rows(spread_ref, head, heads, length):
    here = pl.ds(head, length, stride=heads)
    pieces = [spread_ref[piece, here, :] for piece in range(spread_ref.shape[0])]
    return pieces[0] if len(pieces) == 1 else jnp.concatenate(pieces, axis=1)


def keep_head_rows(spread_ref, head, heads, array):
    length = array.shape[0]
    for piece in range(spread_ref.shape[0]):
        lanes = array[:, piece * LANES : (piece + 1) * LANES]
        spread_ref[piece, pl.ds(head, length, stride=heads), :] = lanes


def reordered(array, order, size):
    return jnp.concatenate([array[start : start + size] for start in order], 0)


def load_kernel(bias_ref, copies_ref, *, rows, heads):
    half = heads // 2
    order = [row * heads + part * half for part in range(2) for row in range(rows)]
    block = reordered(bias_ref[...].astype(jnp.float32), order, half).astype(copies_ref.dtype)
    copies_ref[...] = jnp.broadcast_to(block[None], copies_ref.shape)


def store_kernel(
    received_ref, dq_ref, dk_ref, dv_ref, sum_hbm, dq_hbm, dk_hbm, dv_hbm, sum_ref, sems,
    *, rows, heads
):
    pairs = ((dq_ref, dq_hbm), (dk_ref, dk_hbm), (dv_ref, dv_hbm), (sum_ref, sum_hbm))
    moves = [pltpu.make_async_copy(a, b, sems.at[n]) for n, (a, b) in enumerate(pairs)]
    for move in moves[:3]:
        move.start()
    half = heads // 2
    total = jnp.sum(received_ref[...].astype(jnp.float32), axis=0)
    order = [
        ((1 - part) * rows + row) * half for row in range(rows) for part in range(2)
    ]
    sum_ref[...] = reordered(total, order, half)
    moves[3].start()
    for move in moves:
        move.wait()


def identity(length, dtype):
    rows = lax.broadcasted_iota(jnp.int32, (length, length), 0)
    columns = lax.broadcasted_iota(jnp.int32, (length, length), 1)
    return jnp.where(rows == columns, 1.0, 0.0).astype(dtype)


def joined(parts, width):
    total = parts[0]
    for head in range(1, len(parts)):
        total = jnp.where(head_lanes(total.shape, head, width), parts[head], total)
    return total

def half_kernel(
    bias_ref, q_ref, k_ref, v_ref, g_ref, norm_ref, *refs, heads, first
):
    dqt_before, dk_before, dv_before = (None,) * 3 if first else refs[:3]
    part_ref, dq_ref, dk_ref, dv_ref, spread_ref, kt_ref = refs if first else refs[3:]
    rows, length, channels = q_ref.shape
    width = channels // heads
    half = heads // 2
    scale = width ** (-0.5)
    low = jnp.bfloat16
    every = range(half)
    eye = identity(length, low)
    core = lax.rem(lax.axis_index("row"), 2)
    base = (core if first else 1 - core) * half

    def cut(array, place):
        return array[place * length : (place + 1) * length]

    def stack(array):
        return jnp.concatenate([only_head(array, base + place, width) for place in every], 0)

    spread_rows(spread_ref, bias_ref[...].astype(jnp.float32))
    rows_of = [head_rows(spread_ref, place, half, length).astype(low) for place in every]
    turned = product(eye, jnp.concatenate(rows_of, 0), NT)
    logits = [turned[:, place * length : (place + 1) * length] for place in every]
    sums = [None] * half

    def scored(row):
        return (
            product(stack(k_ref[row]), q_ref[row], NT),
            product(stack(v_ref[row]), g_ref[row], NT),
        )

    def mixed(parts):
        total = parts[0]
        for place in range(1, half):
            lanes = head_lanes(total.shape, base + place, width)
            total = jnp.where(lanes, parts[place], total)
        return total

    depth = min(2, rows)
    ahead = [scored(row) for row in range(depth)]
    for row in range(rows):
        if row + depth < rows:
            ahead.append(scored(row + depth))
        q, g = q_ref[row], g_ref[row]
        s_all, p_all = ahead[row]
        kt_ref[row] = jnp.transpose(k_ref[row])
        w_low, s_low = [], []
        for place in every:
            norms = norm_ref[pl.ds(row * heads + base + place, 1), :]
            weights = jnp.exp(cut(s_all, place) * scale + (logits[place] - norms))
            slopes = cut(p_all, place)
            centre = jnp.sum(weights * slopes, axis=0, keepdims=True)
            grads = weights * (slopes - centre)
            sums[place] = grads if row == 0 else sums[place] + grads
            if row == rows - 1:
                upright = jnp.transpose(sums[place].astype(low)).astype(jnp.float32)
                keep_head_rows(spread_ref, place, half, upright)
            w_low.append(weights.astype(low))
            s_low.append(grads.astype(low))
        dk_all = product(jnp.concatenate(s_low, 0), q)
        dv_all = product(jnp.concatenate(w_low, 0), g)
        dk = (mixed([cut(dk_all, place) for place in every]) * scale).astype(low)
        dv = mixed([cut(dv_all, place) for place in every]).astype(low)
        dqt = []
        for place in every:
            mine = pl.ds(pl.multiple_of((base + place) * width, width), width)
            dqt.append(product(kt_ref[row, mine, :], s_low[place]))
        dqt = (jnp.concatenate(dqt, 0) * scale).astype(low)
        if first:
            dq_ref[row] = dqt
        else:
            lanes = lax.broadcasted_iota(jnp.int32, dk.shape, 1)
            now = (lanes >= base * width) & (lanes < (base + half) * width)
            dk = jnp.where(now, dk, dk_before[row])
            dv = jnp.where(now, dv, dv_before[row])
            before = dqt_before[row]
            low_part = jnp.where(base == 0, dqt, before)
            high_part = jnp.where(base == 0, before, dqt)
            dq_ref[row] = jnp.transpose(jnp.concatenate([low_part, high_part], 0))
        dk_ref[row] = dk
        dv_ref[row] = dv
    for piece in range(length // LANES):
        lanes = spread_ref[piece].astype(part_ref.dtype)
        part_ref[:, piece * LANES : (piece + 1) * LANES] = lanes


def call(kernel, name, outputs, scratch=(), ins=None, outs=None, cost=None):
    def place(space):
        return pl.BlockSpec(memory_space=space)

    specs = {}
    if ins is not None:
        specs["in_specs"] = [place(space) for space in ins]
    if outs is not None:
        specs["out_specs"] = tuple(place(space) for space in outs)
    return pl.pallas_call(
        kernel,
        name=name,
        cost_estimate=cost,
        out_shape=outputs,
        scratch_shapes=scratch,
        compiler_params=pltpu.CompilerParams(vmem_limit_bytes=24 << 20),
        **specs,
    )


def local(queries, keys, values, grads_out, log_norm, bias):
    heads = bias.shape[1]
    rows, length, channels = queries.shape
    devices = lax.axis_size("row")
    shape, f32, bf16 = jax.ShapeDtypeStruct, jnp.float32, jnp.bfloat16
    hbm, vmem, dma = pltpu.HBM, pltpu.VMEM, pltpu.SemaphoreType.DMA
    half = heads // 2
    block = (rows * heads, length)
    flat = (devices * rows * half, length)
    parcel = (devices, rows * half, length)
    chips = (devices // 2,) + block
    pair = shape(queries.shape, bf16)
    sizes = dict(rows=rows, heads=heads)
    siblings = [(device, device ^ 1) for device in range(devices)]
    copies = call(
        functools.partial(load_kernel, **sizes),
        "load",
        shape(chips, bf16),
        cost=pl.CostEstimate(flops=1 << 34, bytes_accessed=1 << 26, transcendentals=0),
    )(bias.reshape(block))
    mine = lax.all_to_all(copies.reshape(parcel), "row", 0, 0).reshape(flat)
    other = lax.ppermute(mine, "row", siblings)
    saved = (queries, keys, values, grads_out, log_norm.reshape(block))
    scratch = (
        vmem((length // LANES, length * half, LANES), f32),
        vmem((rows, channels, length), bf16),
    )
    part, *before = call(
        functools.partial(half_kernel, heads=heads, first=True),
        "first",
        (shape(flat, bf16), shape((rows, channels // 2, length), bf16), pair, pair),
        scratch,
        cost=pl.CostEstimate(flops=1 << 30, bytes_accessed=1 << 20, transcendentals=0),
    )(mine, *saved)
    theirs = lax.ppermute(part, "row", siblings)
    part, *grads = call(
        functools.partial(half_kernel, heads=heads, first=False),
        "second",
        (shape(flat, f32),) + (pair,) * 3,
        scratch,
        cost=pl.CostEstimate(flops=1 << 30, bytes_accessed=1 << 20, transcendentals=0),
    )(other, *saved, *before)
    both = (part + theirs.astype(f32)).astype(bf16)
    received = lax.all_to_all(both.reshape(parcel), "row", 0, 0).reshape(chips)
    bias_grad, *grads = call(
        functools.partial(store_kernel, **sizes),
        "store",
        (shape(block, f32),) + (pair,) * 3,
        (vmem(block, f32), dma((4,))),
        (vmem,) * 4,
        (hbm,) * 4,
    )(received, *grads)
    return (*grads, bias_grad.reshape(bias.shape))


def solution(mesh):
    placed = P(("crop", "row"), None, None)
    return jax.shard_map(
        local, mesh=mesh, in_specs=(placed,) * 6, out_specs=(placed,) * 4, check_vma=False
    )
```

```python
import functools

import jax
import jax.numpy as jnp
from jax import lax
from jax.experimental import pallas as pl
from jax.experimental.pallas import tpu as pltpu
from jax.sharding import PartitionSpec as P

NN = (((1,), (0,)), ((), ()))
NT = (((1,), (1,)), ((), ()))
LANES = 128


def product(left, right, form=NN):
    return lax.dot_general(left, right, form, preferred_element_type=jnp.float32)


def head_lanes(shape, head, width):
    lane = lax.broadcasted_iota(jnp.int32, shape, len(shape) - 1)
    return (lane >= head * width) & (lane < (head + 1) * width)


def only_head(array, head, width):
    return jnp.where(head_lanes(array.shape, head, width), array, jnp.zeros_like(array))


def spread_rows(spread_ref, array):
    for piece in range(array.shape[1] // LANES):
        spread_ref[piece] = array[:, piece * LANES : (piece + 1) * LANES]


def head_rows(spread_ref, head, heads, length):
    here = pl.ds(head, length, stride=heads)
    pieces = [spread_ref[piece, here, :] for piece in range(spread_ref.shape[0])]
    return pieces[0] if len(pieces) == 1 else jnp.concatenate(pieces, axis=1)


def keep_head_rows(spread_ref, head, heads, array):
    length = array.shape[0]
    for piece in range(spread_ref.shape[0]):
        lanes = array[:, piece * LANES : (piece + 1) * LANES]
        spread_ref[piece, pl.ds(head, length, stride=heads), :] = lanes


def reordered(array, order, size):
    return jnp.concatenate([array[start : start + size] for start in order], 0)


def load_kernel(bias_ref, copies_ref, *, rows, heads):
    half = heads // 2
    order = [row * heads + part * half for part in range(2) for row in range(rows)]
    block = reordered(bias_ref[...].astype(jnp.float32), order, half).astype(copies_ref.dtype)
    copies_ref[...] = jnp.broadcast_to(block[None], copies_ref.shape)


def store_kernel(
    received_ref, dq_ref, dk_ref, dv_ref, sum_hbm, dq_hbm, dk_hbm, dv_hbm, sum_ref, sems,
    *, rows, heads
):
    pairs = ((dq_ref, dq_hbm), (dk_ref, dk_hbm), (dv_ref, dv_hbm), (sum_ref, sum_hbm))
    moves = [pltpu.make_async_copy(a, b, sems.at[n]) for n, (a, b) in enumerate(pairs)]
    for move in moves[:3]:
        move.start()
    half = heads // 2
    total = jnp.sum(received_ref[...].astype(jnp.float32), axis=0)
    order = [
        ((1 - part) * rows + row) * half for row in range(rows) for part in range(2)
    ]
    sum_ref[...] = reordered(total, order, half)
    moves[3].start()
    for move in moves:
        move.wait()


def identity(length, dtype):
    rows = lax.broadcasted_iota(jnp.int32, (length, length), 0)
    columns = lax.broadcasted_iota(jnp.int32, (length, length), 1)
    return jnp.where(rows == columns, 1.0, 0.0).astype(dtype)


def joined(parts, width):
    total = parts[0]
    for head in range(1, len(parts)):
        total = jnp.where(head_lanes(total.shape, head, width), parts[head], total)
    return total

def half_kernel(
    bias_ref, q_ref, k_ref, v_ref, g_ref, norm_ref, *refs, heads, first
):
    if first:
        part_ref, dq_ref, dk_ref, dv_ref, w_ref, d_ref, spread_ref, kt_ref = refs
    else:
        dqt_before, dk_before, dv_before, w_ref, d_ref = refs[:5]
        part_ref, dq_ref, dk_ref, dv_ref, spread_ref, kt_ref = refs[5:]
    rows, length, channels = q_ref.shape
    width = channels // heads
    half = heads // 2
    scale = width ** (-0.5)
    low = jnp.bfloat16
    every = range(half)
    eye = identity(length, low)
    core = lax.rem(lax.axis_index("row"), 2)
    base_first = core * half
    base = base_first if first else half - base_first
    kept = rows - w_ref.shape[0]

    def cut(array, place):
        return array[place * length : (place + 1) * length]

    def stack(array):
        return jnp.concatenate([only_head(array, base + place, width) for place in every], 0)

    spread_rows(spread_ref, bias_ref[...].astype(jnp.float32))
    rows_of = [head_rows(spread_ref, place, half, length).astype(low) for place in every]
    turned = product(eye, jnp.concatenate(rows_of, 0), NT)
    logits = [turned[:, place * length : (place + 1) * length] for place in every]
    sums = [None] * half

    def scored(row):
        return (
            product(stack(k_ref[row]), q_ref[row], NT),
            product(stack(v_ref[row]), g_ref[row], NT),
        )

    def mixed(product_all, start):
        total = cut(product_all, 0)
        for place in range(1, half):
            lanes = head_lanes(total.shape, start + place, width)
            total = jnp.where(lanes, cut(product_all, place), total)
        return total

    def graded(row, w_all, s_all, start):
        dk = (mixed(product(s_all, q_ref[row]), start) * scale).astype(low)
        dv = mixed(product(w_all, g_ref[row]), start).astype(low)
        dqt = []
        for place in every:
            mine = pl.ds(pl.multiple_of((start + place) * width, width), width)
            dqt.append(product(kt_ref[row, mine, :], cut(s_all, place)))
        return (jnp.concatenate(dqt, 0) * scale).astype(low), dk, dv

    depth = min(3, rows)
    ahead = [scored(row) for row in range(depth)]
    for row in range(rows):
        if row + depth < rows:
            ahead.append(scored(row + depth))
        s_all, p_all = ahead[row]
        if not first or row < kept:
            kt_ref[row] = jnp.transpose(k_ref[row])
        w_low, s_low = [], []
        for place in every:
            norms = norm_ref[pl.ds(row * heads + base + place, 1), :]
            weights = jnp.exp(cut(s_all, place) * scale + (logits[place] - norms))
            slopes = cut(p_all, place)
            centre = jnp.sum(weights * slopes, axis=0, keepdims=True)
            grads = weights * (slopes - centre)
            sums[place] = grads if row == 0 else sums[place] + grads
            if row == rows - 1:
                upright = jnp.transpose(sums[place].astype(low)).astype(jnp.float32)
                keep_head_rows(spread_ref, place, half, upright)
            w_low.append(weights.astype(low))
            s_low.append(grads.astype(low))
        w_all, s_all = jnp.concatenate(w_low, 0), jnp.concatenate(s_low, 0)
        if first and row >= kept:
            w_ref[row - kept] = w_all
            d_ref[row - kept] = s_all
            continue
        dqt, dk, dv = graded(row, w_all, s_all, base)
        if first:
            dq_ref[row] = dqt
        else:
            if row < kept:
                before, dk_first, dv_first = dqt_before[row], dk_before[row], dv_before[row]
            else:
                late = row - kept
                before, dk_first, dv_first = graded(row, w_ref[late], d_ref[late], base_first)
            lanes = lax.broadcasted_iota(jnp.int32, dk.shape, 1)
            now = (lanes >= base * width) & (lanes < (base + half) * width)
            dk = jnp.where(now, dk, dk_first)
            dv = jnp.where(now, dv, dv_first)
            low_part = jnp.where(base == 0, dqt, before)
            high_part = jnp.where(base == 0, before, dqt)
            dq_ref[row] = jnp.transpose(jnp.concatenate([low_part, high_part], 0))
        dk_ref[row] = dk
        dv_ref[row] = dv
    for piece in range(length // LANES):
        lanes = spread_ref[piece].astype(part_ref.dtype)
        part_ref[:, piece * LANES : (piece + 1) * LANES] = lanes


def call(kernel, name, outputs, scratch=(), ins=None, outs=None, cost=None):
    def place(space):
        return pl.BlockSpec(memory_space=space)

    specs = {}
    if ins is not None:
        specs["in_specs"] = [place(space) for space in ins]
    if outs is not None:
        specs["out_specs"] = tuple(place(space) for space in outs)
    return pl.pallas_call(
        kernel,
        name=name,
        cost_estimate=cost,
        out_shape=outputs,
        scratch_shapes=scratch,
        compiler_params=pltpu.CompilerParams(vmem_limit_bytes=24 << 20),
        **specs,
    )


def local(queries, keys, values, grads_out, log_norm, bias):
    heads = bias.shape[1]
    rows, length, channels = queries.shape
    devices = lax.axis_size("row")
    shape, f32, bf16 = jax.ShapeDtypeStruct, jnp.float32, jnp.bfloat16
    hbm, vmem, dma = pltpu.HBM, pltpu.VMEM, pltpu.SemaphoreType.DMA
    half = heads // 2
    block = (rows * heads, length)
    flat = (devices * rows * half, length)
    parcel = (devices, rows * half, length)
    chips = (devices // 2,) + block
    pair = shape(queries.shape, bf16)
    sizes = dict(rows=rows, heads=heads)
    siblings = [(device, device ^ 1) for device in range(devices)]
    copies = call(
        functools.partial(load_kernel, **sizes),
        "load",
        shape(chips, bf16),
        cost=pl.CostEstimate(flops=1 << 34, bytes_accessed=1 << 26, transcendentals=0),
    )(bias.reshape(block))
    mine = lax.all_to_all(copies.reshape(parcel), "row", 0, 0).reshape(flat)
    other = lax.ppermute(mine, "row", siblings)
    saved = (queries, keys, values, grads_out, log_norm.reshape(block))
    scratch = (
        vmem((length // LANES, length * half, LANES), f32),
        vmem((rows, channels, length), bf16),
    )
    late = min(2, rows - 1)
    kept = rows - late
    done = [shape((kept, channels // 2, length), bf16)]
    done += [shape((kept, length, channels), bf16)] * 2
    held = shape((late, half * length, length), bf16)
    part, *before = call(
        functools.partial(half_kernel, heads=heads, first=True),
        "first",
        (shape(flat, bf16), *done, held, held),
        scratch,
        cost=pl.CostEstimate(flops=1 << 30, bytes_accessed=1 << 20, transcendentals=0),
    )(mine, *saved)
    theirs = lax.ppermute(part, "row", siblings)
    part, *grads = call(
        functools.partial(half_kernel, heads=heads, first=False),
        "second",
        (shape(flat, f32),) + (pair,) * 3,
        scratch,
        cost=pl.CostEstimate(flops=1 << 30, bytes_accessed=1 << 20, transcendentals=0),
    )(other, *saved, *before)
    both = (part + theirs.astype(f32)).astype(bf16)
    received = lax.all_to_all(both.reshape(parcel), "row", 0, 0).reshape(chips)
    bias_grad, *grads = call(
        functools.partial(store_kernel, **sizes),
        "store",
        (shape(block, f32),) + (pair,) * 3,
        (vmem(block, f32), dma((4,))),
        (vmem,) * 4,
        (hbm,) * 4,
    )(received, *grads)
    return (*grads, bias_grad.reshape(bias.shape))


def solution(mesh):
    placed = P(("crop", "row"), None, None)
    return jax.shard_map(
        local, mesh=mesh, in_specs=(placed,) * 6, out_specs=(placed,) * 4, check_vma=False
    )
```

```python
import functools

import jax
import jax.numpy as jnp
from jax import lax
from jax.experimental import pallas as pl
from jax.experimental.pallas import tpu as pltpu
from jax.sharding import PartitionSpec as P

NN = (((1,), (0,)), ((), ()))
NT = (((1,), (1,)), ((), ()))
LANES = 128


def product(left, right, form=NN):
    return lax.dot_general(left, right, form, preferred_element_type=jnp.float32)


def head_lanes(shape, head, width):
    lane = lax.broadcasted_iota(jnp.int32, shape, len(shape) - 1)
    return (lane >= head * width) & (lane < (head + 1) * width)


def only_head(array, head, width):
    return jnp.where(head_lanes(array.shape, head, width), array, jnp.zeros_like(array))


def spread_rows(spread_ref, array):
    for piece in range(array.shape[1] // LANES):
        spread_ref[piece] = array[:, piece * LANES : (piece + 1) * LANES]


def head_rows(spread_ref, head, heads, length):
    here = pl.ds(head, length, stride=heads)
    pieces = [spread_ref[piece, here, :] for piece in range(spread_ref.shape[0])]
    return pieces[0] if len(pieces) == 1 else jnp.concatenate(pieces, axis=1)


def keep_head_rows(spread_ref, head, heads, array):
    length = array.shape[0]
    for piece in range(spread_ref.shape[0]):
        lanes = array[:, piece * LANES : (piece + 1) * LANES]
        spread_ref[piece, pl.ds(head, length, stride=heads), :] = lanes


def reordered(array, order, size):
    return jnp.concatenate([array[start : start + size] for start in order], 0)


def load_kernel(bias_ref, copies_ref, *, rows, heads):
    half = heads // 2
    order = [row * heads + part * half for part in range(2) for row in range(rows)]
    block = reordered(bias_ref[...].astype(jnp.float32), order, half).astype(copies_ref.dtype)
    copies_ref[...] = jnp.broadcast_to(block[None], copies_ref.shape)


def store_kernel(
    received_ref, dq_ref, dk_ref, dv_ref, sum_hbm, dq_hbm, dk_hbm, dv_hbm, sum_ref, sems,
    *, rows, heads
):
    pairs = ((dq_ref, dq_hbm), (dk_ref, dk_hbm), (dv_ref, dv_hbm), (sum_ref, sum_hbm))
    moves = [pltpu.make_async_copy(a, b, sems.at[n]) for n, (a, b) in enumerate(pairs)]
    for move in moves[:3]:
        move.start()
    half = heads // 2
    total = jnp.sum(received_ref[...].astype(jnp.float32), axis=0)
    order = [
        ((1 - part) * rows + row) * half for row in range(rows) for part in range(2)
    ]
    sum_ref[...] = reordered(total, order, half)
    moves[3].start()
    for move in moves:
        move.wait()


def identity(length, dtype):
    rows = lax.broadcasted_iota(jnp.int32, (length, length), 0)
    columns = lax.broadcasted_iota(jnp.int32, (length, length), 1)
    return jnp.where(rows == columns, 1.0, 0.0).astype(dtype)


def joined(parts, width):
    total = parts[0]
    for head in range(1, len(parts)):
        total = jnp.where(head_lanes(total.shape, head, width), parts[head], total)
    return total

def half_kernel(
    bias_ref, q_ref, k_ref, v_ref, g_ref, norm_ref, *refs, heads, first
):
    if first:
        part_ref, dq_ref, dk_ref, dv_ref, w_ref, d_ref, spread_ref, kt_ref = refs
    else:
        dqt_before, dk_before, dv_before, w_ref, d_ref = refs[:5]
        part_ref, dq_ref, dk_ref, dv_ref, spread_ref, kt_ref = refs[5:]
    rows, length, channels = q_ref.shape
    width = channels // heads
    half = heads // 2
    scale = width ** (-0.5)
    low = jnp.bfloat16
    every = range(half)
    eye = identity(length, low)
    core = lax.rem(lax.axis_index("row"), 2)
    base_first = core * half
    base = base_first if first else half - base_first
    kept = rows - w_ref.shape[0]

    def cut(array, place):
        return array[place * length : (place + 1) * length]

    def stack(array):
        return jnp.concatenate([only_head(array, base + place, width) for place in every], 0)

    spread_rows(spread_ref, bias_ref[...].astype(jnp.float32))
    rows_of = [head_rows(spread_ref, place, half, length).astype(low) for place in every]
    if first:
        logits = [jnp.transpose(rows_of[place]).astype(jnp.float32) for place in every]
    else:
        turned = product(eye, jnp.concatenate(rows_of, 0), NT)
        logits = [turned[:, place * length : (place + 1) * length] for place in every]
    sums = [None] * half

    def scored(row):
        return (
            product(stack(k_ref[row]), q_ref[row], NT),
            product(stack(v_ref[row]), g_ref[row], NT),
        )

    def mixed(product_all, start):
        total = cut(product_all, 0)
        for place in range(1, half):
            lanes = head_lanes(total.shape, start + place, width)
            total = jnp.where(lanes, cut(product_all, place), total)
        return total

    def graded(row, w_all, s_all, start):
        dk = (mixed(product(s_all, q_ref[row]), start) * scale).astype(low)
        dv = mixed(product(w_all, g_ref[row]), start).astype(low)
        dqt = []
        for place in every:
            mine = pl.ds(pl.multiple_of((start + place) * width, width), width)
            dqt.append(product(kt_ref[row, mine, :], cut(s_all, place)))
        return (jnp.concatenate(dqt, 0) * scale).astype(low), dk, dv

    depth = min(3, rows)
    ahead = [scored(row) for row in range(depth)]
    for row in range(rows):
        if row + depth < rows:
            ahead.append(scored(row + depth))
        s_all, p_all = ahead[row]
        if not first or row < kept:
            kt_ref[row] = jnp.transpose(k_ref[row])
        w_low, s_low = [], []
        for place in every:
            norms = norm_ref[pl.ds(row * heads + base + place, 1), :]
            weights = jnp.exp(cut(s_all, place) * scale + (logits[place] - norms))
            slopes = cut(p_all, place)
            centre = jnp.sum(weights * slopes, axis=0, keepdims=True)
            grads = weights * (slopes - centre)
            sums[place] = grads if row == 0 else sums[place] + grads
            if row == rows - 1:
                upright = jnp.transpose(sums[place].astype(low)).astype(jnp.float32)
                keep_head_rows(spread_ref, place, half, upright)
            w_low.append(weights.astype(low))
            s_low.append(grads.astype(low))
        w_all, s_all = jnp.concatenate(w_low, 0), jnp.concatenate(s_low, 0)
        if first and row >= kept:
            w_ref[row - kept] = w_all
            d_ref[row - kept] = s_all
            continue
        dqt, dk, dv = graded(row, w_all, s_all, base)
        if first:
            dq_ref[row] = dqt
        else:
            if row < kept:
                before, dk_first, dv_first = dqt_before[row], dk_before[row], dv_before[row]
            else:
                late = row - kept
                before, dk_first, dv_first = graded(row, w_ref[late], d_ref[late], base_first)
            lanes = lax.broadcasted_iota(jnp.int32, dk.shape, 1)
            now = (lanes >= base * width) & (lanes < (base + half) * width)
            dk = jnp.where(now, dk, dk_first)
            dv = jnp.where(now, dv, dv_first)
            low_part = jnp.where(base == 0, dqt, before)
            high_part = jnp.where(base == 0, before, dqt)
            dq_ref[row] = jnp.transpose(jnp.concatenate([low_part, high_part], 0))
        dk_ref[row] = dk
        dv_ref[row] = dv
    for piece in range(length // LANES):
        lanes = spread_ref[piece].astype(part_ref.dtype)
        part_ref[:, piece * LANES : (piece + 1) * LANES] = lanes


def call(kernel, name, outputs, scratch=(), ins=None, outs=None, cost=None):
    def place(space):
        return pl.BlockSpec(memory_space=space)

    specs = {}
    if ins is not None:
        specs["in_specs"] = [place(space) for space in ins]
    if outs is not None:
        specs["out_specs"] = tuple(place(space) for space in outs)
    return pl.pallas_call(
        kernel,
        name=name,
        cost_estimate=cost,
        out_shape=outputs,
        scratch_shapes=scratch,
        compiler_params=pltpu.CompilerParams(vmem_limit_bytes=24 << 20),
        **specs,
    )


def local(queries, keys, values, grads_out, log_norm, bias):
    heads = bias.shape[1]
    rows, length, channels = queries.shape
    devices = lax.axis_size("row")
    shape, f32, bf16 = jax.ShapeDtypeStruct, jnp.float32, jnp.bfloat16
    hbm, vmem, dma = pltpu.HBM, pltpu.VMEM, pltpu.SemaphoreType.DMA
    half = heads // 2
    block = (rows * heads, length)
    flat = (devices * rows * half, length)
    parcel = (devices, rows * half, length)
    chips = (devices // 2,) + block
    pair = shape(queries.shape, bf16)
    sizes = dict(rows=rows, heads=heads)
    siblings = [(device, device ^ 1) for device in range(devices)]
    copies = call(
        functools.partial(load_kernel, **sizes),
        "load",
        shape(chips, bf16),
        cost=pl.CostEstimate(flops=1 << 34, bytes_accessed=1 << 26, transcendentals=0),
    )(bias.reshape(block))
    mine = lax.all_to_all(copies.reshape(parcel), "row", 0, 0).reshape(flat)
    other = lax.ppermute(mine, "row", siblings)
    saved = (queries, keys, values, grads_out, log_norm.reshape(block))
    scratch = (
        vmem((length // LANES, length * half, LANES), f32),
        vmem((rows, channels, length), bf16),
    )
    late = min(2, rows - 1)
    kept = rows - late
    done = [shape((kept, channels // 2, length), bf16)]
    done += [shape((kept, length, channels), bf16)] * 2
    held = shape((late, half * length, length), bf16)
    part, *before = call(
        functools.partial(half_kernel, heads=heads, first=True),
        "first",
        (shape(flat, bf16), *done, held, held),
        scratch,
        cost=pl.CostEstimate(flops=1 << 30, bytes_accessed=1 << 20, transcendentals=0),
    )(mine, *saved)
    theirs = lax.ppermute(part, "row", siblings)
    part, *grads = call(
        functools.partial(half_kernel, heads=heads, first=False),
        "second",
        (shape(flat, f32),) + (pair,) * 3,
        scratch,
        cost=pl.CostEstimate(flops=1 << 30, bytes_accessed=1 << 20, transcendentals=0),
    )(other, *saved, *before)
    both = (part + theirs.astype(f32)).astype(bf16)
    received = lax.all_to_all(both.reshape(parcel), "row", 0, 0).reshape(chips)
    bias_grad, *grads = call(
        functools.partial(store_kernel, **sizes),
        "store",
        (shape(block, f32),) + (pair,) * 3,
        (vmem(block, f32), dma((4,))),
        (vmem,) * 4,
        (hbm,) * 4,
    )(received, *grads)
    return (*grads, bias_grad.reshape(bias.shape))


def solution(mesh):
    placed = P(("crop", "row"), None, None)
    return jax.shard_map(
        local, mesh=mesh, in_specs=(placed,) * 6, out_specs=(placed,) * 4, check_vma=False
    )
```

```python
import functools

import jax
import jax.numpy as jnp
from jax import lax
from jax.experimental import pallas as pl
from jax.experimental.pallas import tpu as pltpu
from jax.sharding import PartitionSpec as P

NN = (((1,), (0,)), ((), ()))
NT = (((1,), (1,)), ((), ()))
LANES = 128


def product(left, right, form=NN):
    return lax.dot_general(left, right, form, preferred_element_type=jnp.float32)


def head_lanes(shape, head, width):
    lane = lax.broadcasted_iota(jnp.int32, shape, len(shape) - 1)
    return (lane >= head * width) & (lane < (head + 1) * width)


def only_head(array, head, width):
    return jnp.where(head_lanes(array.shape, head, width), array, jnp.zeros_like(array))


def spread_rows(spread_ref, array):
    for piece in range(array.shape[1] // LANES):
        spread_ref[piece] = array[:, piece * LANES : (piece + 1) * LANES]


def head_rows(spread_ref, head, heads, length):
    here = pl.ds(head, length, stride=heads)
    pieces = [spread_ref[piece, here, :] for piece in range(spread_ref.shape[0])]
    return pieces[0] if len(pieces) == 1 else jnp.concatenate(pieces, axis=1)


def keep_head_rows(spread_ref, head, heads, array):
    length = array.shape[0]
    for piece in range(spread_ref.shape[0]):
        lanes = array[:, piece * LANES : (piece + 1) * LANES]
        spread_ref[piece, pl.ds(head, length, stride=heads), :] = lanes


def reordered(array, order, size):
    return jnp.concatenate([array[start : start + size] for start in order], 0)


def load_kernel(bias_ref, copies_ref, *, rows, heads):
    half = heads // 2
    order = [row * heads + part * half for part in range(2) for row in range(rows)]
    block = reordered(bias_ref[...].astype(jnp.float32), order, half).astype(copies_ref.dtype)
    copies_ref[...] = jnp.broadcast_to(block[None], copies_ref.shape)


def store_kernel(
    received_ref, dq_ref, dk_ref, dv_ref, sum_hbm, dq_hbm, dk_hbm, dv_hbm, sum_ref, sems,
    *, rows, heads
):
    pairs = ((dq_ref, dq_hbm), (dk_ref, dk_hbm), (dv_ref, dv_hbm), (sum_ref, sum_hbm))
    moves = [pltpu.make_async_copy(a, b, sems.at[n]) for n, (a, b) in enumerate(pairs)]
    for move in moves[:3]:
        move.start()
    half = heads // 2
    total = jnp.sum(received_ref[...].astype(jnp.float32), axis=0)
    order = [
        ((1 - part) * rows + row) * half for row in range(rows) for part in range(2)
    ]
    sum_ref[...] = reordered(total, order, half)
    moves[3].start()
    for move in moves:
        move.wait()


def identity(length, dtype):
    rows = lax.broadcasted_iota(jnp.int32, (length, length), 0)
    columns = lax.broadcasted_iota(jnp.int32, (length, length), 1)
    return jnp.where(rows == columns, 1.0, 0.0).astype(dtype)


def joined(parts, width):
    total = parts[0]
    for head in range(1, len(parts)):
        total = jnp.where(head_lanes(total.shape, head, width), parts[head], total)
    return total

def half_kernel(
    bias_ref, q_ref, k_ref, v_ref, g_ref, norm_ref, *refs, heads, first
):
    if first:
        part_ref, dq_ref, dk_ref, dv_ref, w_ref, d_ref, spread_ref, kt_ref = refs
    else:
        dqt_before, dk_before, dv_before, w_ref, d_ref = refs[:5]
        part_ref, dq_ref, dk_ref, dv_ref, spread_ref, kt_ref = refs[5:]
    rows, length, channels = q_ref.shape
    width = channels // heads
    half = heads // 2
    scale = width ** (-0.5)
    low = jnp.bfloat16
    every = range(half)
    eye = identity(length, low)
    core = lax.rem(lax.axis_index("row"), 2)
    base_first = core * half
    base = base_first if first else half - base_first
    kept = rows - w_ref.shape[0]

    def cut(array, place):
        return array[place * length : (place + 1) * length]

    def stack(array):
        return jnp.concatenate([only_head(array, base + place, width) for place in every], 0)

    spread_rows(spread_ref, bias_ref[...].astype(jnp.float32))
    rows_of = [head_rows(spread_ref, place, half, length).astype(low) for place in every]
    if first:
        logits = [jnp.transpose(rows_of[place]).astype(jnp.float32) for place in every]
    else:
        turned = product(eye, jnp.concatenate(rows_of, 0), NT)
        logits = [turned[:, place * length : (place + 1) * length] for place in every]
    sums = [None] * half

    def scored(row):
        return (
            product(stack(k_ref[row]), q_ref[row], NT),
            product(stack(v_ref[row]), g_ref[row], NT),
        )

    def mixed(product_all, start):
        total = cut(product_all, 0)
        for place in range(1, half):
            lanes = head_lanes(total.shape, start + place, width)
            total = jnp.where(lanes, cut(product_all, place), total)
        return total

    def graded(row, w_all, s_all, start):
        dk = (mixed(product(s_all, q_ref[row]), start) * scale).astype(low)
        dv = mixed(product(w_all, g_ref[row]), start).astype(low)
        dqt = []
        for place in every:
            mine = pl.ds(pl.multiple_of((start + place) * width, width), width)
            dqt.append(product(kt_ref[row, mine, :], cut(s_all, place)))
        return (jnp.concatenate(dqt, 0) * scale).astype(low), dk, dv

    depth = min(3, rows)
    ahead = [scored(row) for row in range(depth)]
    for row in range(rows):
        if row + depth < rows:
            ahead.append(scored(row + depth))
        s_all, p_all = ahead[row]
        if not first or row < kept:
            kt_ref[row] = jnp.transpose(k_ref[row])
        w_low, s_low = [], []
        for place in every:
            norms = norm_ref[pl.ds(row * heads + base + place, 1), :]
            weights = jnp.exp(cut(s_all, place) * scale + (logits[place] - norms))
            slopes = cut(p_all, place)
            centre = jnp.sum(weights * slopes, axis=0, keepdims=True)
            grads = weights * (slopes - centre)
            sums[place] = grads if row == 0 else sums[place] + grads
            if row == rows - 1:
                upright = jnp.transpose(sums[place].astype(low)).astype(jnp.float32)
                keep_head_rows(spread_ref, place, half, upright)
            w_low.append(weights.astype(low))
            s_low.append(grads.astype(low))
        w_all, s_all = jnp.concatenate(w_low, 0), jnp.concatenate(s_low, 0)
        if first and row >= kept:
            w_ref[row - kept] = w_all
            d_ref[row - kept] = s_all
            continue
        dqt, dk, dv = graded(row, w_all, s_all, base)
        if first:
            dq_ref[row] = dqt
        else:
            if row < kept:
                before, dk_first, dv_first = dqt_before[row], dk_before[row], dv_before[row]
            else:
                late = row - kept
                before, dk_first, dv_first = graded(row, w_ref[late], d_ref[late], base_first)
            lanes = lax.broadcasted_iota(jnp.int32, dk.shape, 1)
            now = (lanes >= base * width) & (lanes < (base + half) * width)
            dk = jnp.where(now, dk, dk_first)
            dv = jnp.where(now, dv, dv_first)
            low_part = jnp.where(base == 0, dqt, before)
            high_part = jnp.where(base == 0, before, dqt)
            dq_ref[row] = jnp.transpose(jnp.concatenate([low_part, high_part], 0))
        dk_ref[row] = dk
        dv_ref[row] = dv
    for piece in range(length // LANES):
        lanes = spread_ref[piece].astype(part_ref.dtype)
        part_ref[:, piece * LANES : (piece + 1) * LANES] = lanes


def call(kernel, name, outputs, scratch=(), ins=None, outs=None, cost=None):
    def place(space):
        return pl.BlockSpec(memory_space=space)

    specs = {}
    if ins is not None:
        specs["in_specs"] = [place(space) for space in ins]
    if outs is not None:
        specs["out_specs"] = tuple(place(space) for space in outs)
    return pl.pallas_call(
        kernel,
        name=name,
        cost_estimate=cost,
        out_shape=outputs,
        scratch_shapes=scratch,
        compiler_params=pltpu.CompilerParams(vmem_limit_bytes=24 << 20),
        **specs,
    )


def local(queries, keys, values, grads_out, log_norm, bias):
    heads = bias.shape[1]
    rows, length, channels = queries.shape
    devices = lax.axis_size("row")
    shape, f32, bf16 = jax.ShapeDtypeStruct, jnp.float32, jnp.bfloat16
    hbm, vmem, dma = pltpu.HBM, pltpu.VMEM, pltpu.SemaphoreType.DMA
    half = heads // 2
    block = (rows * heads, length)
    flat = (devices * rows * half, length)
    parcel = (devices, rows * half, length)
    chips = (devices // 2,) + block
    pair = shape(queries.shape, bf16)
    sizes = dict(rows=rows, heads=heads)
    siblings = [(device, device ^ 1) for device in range(devices)]
    copies = call(
        functools.partial(load_kernel, **sizes),
        "load",
        shape(chips, bf16),
        cost=pl.CostEstimate(flops=1 << 34, bytes_accessed=1 << 26, transcendentals=0),
    )(bias.reshape(block))
    mine = lax.all_to_all(copies.reshape(parcel), "row", 0, 0).reshape(flat)
    other = lax.ppermute(mine, "row", siblings)
    saved = (queries, keys, values, grads_out, log_norm.reshape(block))
    scratch = (
        vmem((length // LANES, length * half, LANES), f32),
        vmem((rows, channels, length), bf16),
    )
    late = min(1, rows - 1)
    kept = rows - late
    done = [shape((kept, channels // 2, length), bf16)]
    done += [shape((kept, length, channels), bf16)] * 2
    held = shape((late, half * length, length), bf16)
    part, *before = call(
        functools.partial(half_kernel, heads=heads, first=True),
        "first",
        (shape(flat, bf16), *done, held, held),
        scratch,
        cost=pl.CostEstimate(flops=1 << 30, bytes_accessed=1 << 20, transcendentals=0),
    )(mine, *saved)
    theirs = lax.ppermute(part, "row", siblings)
    part, *grads = call(
        functools.partial(half_kernel, heads=heads, first=False),
        "second",
        (shape(flat, f32),) + (pair,) * 3,
        scratch,
        cost=pl.CostEstimate(flops=1 << 30, bytes_accessed=1 << 20, transcendentals=0),
    )(other, *saved, *before)
    both = (part + theirs.astype(f32)).astype(bf16)
    received = lax.all_to_all(both.reshape(parcel), "row", 0, 0).reshape(chips)
    bias_grad, *grads = call(
        functools.partial(store_kernel, **sizes),
        "store",
        (shape(block, f32),) + (pair,) * 3,
        (vmem(block, f32), dma((4,))),
        (vmem,) * 4,
        (hbm,) * 4,
    )(received, *grads)
    return (*grads, bias_grad.reshape(bias.shape))


def solution(mesh):
    placed = P(("crop", "row"), None, None)
    return jax.shard_map(
        local, mesh=mesh, in_specs=(placed,) * 6, out_specs=(placed,) * 4, check_vma=False
    )
```

```python
import functools

import jax
import jax.numpy as jnp
from jax import lax
from jax.experimental import pallas as pl
from jax.experimental.pallas import tpu as pltpu
from jax.sharding import PartitionSpec as P

NN = (((1,), (0,)), ((), ()))
NT = (((1,), (1,)), ((), ()))
LANES = 128


def product(left, right, form=NN):
    return lax.dot_general(left, right, form, preferred_element_type=jnp.float32)


def head_lanes(shape, head, width):
    lane = lax.broadcasted_iota(jnp.int32, shape, len(shape) - 1)
    return (lane >= head * width) & (lane < (head + 1) * width)


def only_head(array, head, width):
    return jnp.where(head_lanes(array.shape, head, width), array, jnp.zeros_like(array))


def spread_rows(spread_ref, array):
    for piece in range(array.shape[1] // LANES):
        spread_ref[piece] = array[:, piece * LANES : (piece + 1) * LANES]


def head_rows(spread_ref, head, heads, length):
    here = pl.ds(head, length, stride=heads)
    pieces = [spread_ref[piece, here, :] for piece in range(spread_ref.shape[0])]
    return pieces[0] if len(pieces) == 1 else jnp.concatenate(pieces, axis=1)


def keep_head_rows(spread_ref, head, heads, array):
    length = array.shape[0]
    for piece in range(spread_ref.shape[0]):
        lanes = array[:, piece * LANES : (piece + 1) * LANES]
        spread_ref[piece, pl.ds(head, length, stride=heads), :] = lanes


def reordered(array, order, size):
    return jnp.concatenate([array[start : start + size] for start in order], 0)


def load_kernel(bias_ref, copies_ref, *, rows, heads):
    half = heads // 2
    order = [row * heads + part * half for part in range(2) for row in range(rows)]
    block = reordered(bias_ref[...].astype(jnp.float32), order, half).astype(copies_ref.dtype)
    copies_ref[...] = jnp.broadcast_to(block[None], copies_ref.shape)


def store_kernel(
    received_ref, dq_ref, dk_ref, dv_ref, sum_hbm, dq_hbm, dk_hbm, dv_hbm, sum_ref, sems,
    *, rows, heads
):
    pairs = ((dq_ref, dq_hbm), (dk_ref, dk_hbm), (dv_ref, dv_hbm), (sum_ref, sum_hbm))
    moves = [pltpu.make_async_copy(a, b, sems.at[n]) for n, (a, b) in enumerate(pairs)]
    for move in moves[:3]:
        move.start()
    half = heads // 2
    total = jnp.sum(received_ref[...].astype(jnp.float32), axis=0)
    order = [
        ((1 - part) * rows + row) * half for row in range(rows) for part in range(2)
    ]
    sum_ref[...] = reordered(total, order, half)
    moves[3].start()
    for move in moves:
        move.wait()


def identity(length, dtype):
    rows = lax.broadcasted_iota(jnp.int32, (length, length), 0)
    columns = lax.broadcasted_iota(jnp.int32, (length, length), 1)
    return jnp.where(rows == columns, 1.0, 0.0).astype(dtype)


def joined(parts, width):
    total = parts[0]
    for head in range(1, len(parts)):
        total = jnp.where(head_lanes(total.shape, head, width), parts[head], total)
    return total

def half_kernel(
    bias_ref, q_ref, k_ref, v_ref, g_ref, norm_ref, *refs, heads, first
):
    if first:
        part_ref, dq_ref, dk_ref, dv_ref, w_ref, d_ref, spread_ref, kt_ref = refs
    else:
        dqt_before, dk_before, dv_before, w_ref, d_ref = refs[:5]
        part_ref, dq_ref, dk_ref, dv_ref, spread_ref, kt_ref = refs[5:]
    rows, length, channels = q_ref.shape
    width = channels // heads
    half = heads // 2
    scale = width ** (-0.5)
    low = jnp.bfloat16
    every = range(half)
    eye = identity(length, low)
    core = lax.rem(lax.axis_index("row"), 2)
    base_first = core * half
    base = base_first if first else half - base_first
    kept = rows - w_ref.shape[0]

    def cut(array, place):
        return array[place * length : (place + 1) * length]

    def stack(array):
        return jnp.concatenate([only_head(array, base + place, width) for place in every], 0)

    spread_rows(spread_ref, bias_ref[...].astype(jnp.float32))
    rows_of = [head_rows(spread_ref, place, half, length).astype(low) for place in every]
    if first:
        logits = [jnp.transpose(rows_of[place]).astype(jnp.float32) for place in every]
    else:
        turned = product(eye, jnp.concatenate(rows_of, 0), NT)
        logits = [turned[:, place * length : (place + 1) * length] for place in every]
    sums = [None] * half

    def scored(row):
        return (
            product(stack(k_ref[row]), q_ref[row], NT),
            product(stack(v_ref[row]), g_ref[row], NT),
        )

    def mixed(product_all, start):
        total = cut(product_all, 0)
        for place in range(1, half):
            lanes = head_lanes(total.shape, start + place, width)
            total = jnp.where(lanes, cut(product_all, place), total)
        return total

    def graded(row, w_all, s_all, start):
        dk = (mixed(product(s_all, q_ref[row]), start) * scale).astype(low)
        dv = mixed(product(w_all, g_ref[row]), start).astype(low)
        dqt = []
        for place in every:
            mine = pl.ds(pl.multiple_of((start + place) * width, width), width)
            dqt.append(product(kt_ref[row, mine, :], cut(s_all, place)))
        return (jnp.concatenate(dqt, 0) * scale).astype(low), dk, dv

    depth = min(3, rows)
    ahead = [scored(row) for row in range(depth)]
    for row in range(rows):
        if row + depth < rows:
            ahead.append(scored(row + depth))
        s_all, p_all = ahead[row]
        if not first or row < kept:
            kt_ref[row] = jnp.transpose(k_ref[row])
        w_low, s_low = [], []
        for place in every:
            norms = norm_ref[pl.ds(row * heads + base + place, 1), :]
            weights = jnp.exp(cut(s_all, place) * scale + (logits[place] - norms))
            slopes = cut(p_all, place)
            centre = jnp.sum(weights * slopes, axis=0, keepdims=True)
            grads = weights * (slopes - centre)
            sums[place] = grads if row == 0 else sums[place] + grads
            if row == rows - 1:
                sent = sums[place].astype(low) if first else sums[place]
                upright = jnp.transpose(sent).astype(jnp.float32)
                keep_head_rows(spread_ref, place, half, upright)
            w_low.append(weights.astype(low))
            s_low.append(grads.astype(low))
        w_all, s_all = jnp.concatenate(w_low, 0), jnp.concatenate(s_low, 0)
        if first and row >= kept:
            w_ref[row - kept] = w_all
            d_ref[row - kept] = s_all
            continue
        dqt, dk, dv = graded(row, w_all, s_all, base)
        if first:
            dq_ref[row] = dqt
        else:
            if row < kept:
                before, dk_first, dv_first = dqt_before[row], dk_before[row], dv_before[row]
            else:
                late = row - kept
                before, dk_first, dv_first = graded(row, w_ref[late], d_ref[late], base_first)
            lanes = lax.broadcasted_iota(jnp.int32, dk.shape, 1)
            now = (lanes >= base * width) & (lanes < (base + half) * width)
            dk = jnp.where(now, dk, dk_first)
            dv = jnp.where(now, dv, dv_first)
            low_part = jnp.where(base == 0, dqt, before)
            high_part = jnp.where(base == 0, before, dqt)
            dq_ref[row] = jnp.transpose(jnp.concatenate([low_part, high_part], 0))
        dk_ref[row] = dk
        dv_ref[row] = dv
    for piece in range(length // LANES):
        lanes = spread_ref[piece].astype(part_ref.dtype)
        part_ref[:, piece * LANES : (piece + 1) * LANES] = lanes


def call(kernel, name, outputs, scratch=(), ins=None, outs=None, cost=None):
    def place(space):
        return pl.BlockSpec(memory_space=space)

    specs = {}
    if ins is not None:
        specs["in_specs"] = [place(space) for space in ins]
    if outs is not None:
        specs["out_specs"] = tuple(place(space) for space in outs)
    return pl.pallas_call(
        kernel,
        name=name,
        cost_estimate=cost,
        out_shape=outputs,
        scratch_shapes=scratch,
        compiler_params=pltpu.CompilerParams(vmem_limit_bytes=24 << 20),
        **specs,
    )


def local(queries, keys, values, grads_out, log_norm, bias):
    heads = bias.shape[1]
    rows, length, channels = queries.shape
    devices = lax.axis_size("row")
    shape, f32, bf16 = jax.ShapeDtypeStruct, jnp.float32, jnp.bfloat16
    hbm, vmem, dma = pltpu.HBM, pltpu.VMEM, pltpu.SemaphoreType.DMA
    half = heads // 2
    block = (rows * heads, length)
    flat = (devices * rows * half, length)
    parcel = (devices, rows * half, length)
    chips = (devices // 2,) + block
    pair = shape(queries.shape, bf16)
    sizes = dict(rows=rows, heads=heads)
    siblings = [(device, device ^ 1) for device in range(devices)]
    copies = call(
        functools.partial(load_kernel, **sizes),
        "load",
        shape(chips, bf16),
        cost=pl.CostEstimate(flops=1 << 34, bytes_accessed=1 << 26, transcendentals=0),
    )(bias.reshape(block))
    mine = lax.all_to_all(copies.reshape(parcel), "row", 0, 0).reshape(flat)
    other = lax.ppermute(mine, "row", siblings)
    saved = (queries, keys, values, grads_out, log_norm.reshape(block))
    scratch = (
        vmem((length // LANES, length * half, LANES), f32),
        vmem((rows, channels, length), bf16),
    )
    late = min(1, rows - 1)
    kept = rows - late
    done = [shape((kept, channels // 2, length), bf16)]
    done += [shape((kept, length, channels), bf16)] * 2
    held = shape((late, half * length, length), bf16)
    part, *before = call(
        functools.partial(half_kernel, heads=heads, first=True),
        "first",
        (shape(flat, bf16), *done, held, held),
        scratch,
        cost=pl.CostEstimate(flops=1 << 30, bytes_accessed=1 << 20, transcendentals=0),
    )(mine, *saved)
    theirs = lax.ppermute(part, "row", siblings)
    part, *grads = call(
        functools.partial(half_kernel, heads=heads, first=False),
        "second",
        (shape(flat, f32),) + (pair,) * 3,
        scratch,
        cost=pl.CostEstimate(flops=1 << 30, bytes_accessed=1 << 20, transcendentals=0),
    )(other, *saved, *before)
    both = (part + theirs.astype(f32)).astype(bf16)
    received = lax.all_to_all(both.reshape(parcel), "row", 0, 0).reshape(chips)
    bias_grad, *grads = call(
        functools.partial(store_kernel, **sizes),
        "store",
        (shape(block, f32),) + (pair,) * 3,
        (vmem(block, f32), dma((4,))),
        (vmem,) * 4,
        (hbm,) * 4,
    )(received, *grads)
    return (*grads, bias_grad.reshape(bias.shape))


def solution(mesh):
    placed = P(("crop", "row"), None, None)
    return jax.shard_map(
        local, mesh=mesh, in_specs=(placed,) * 6, out_specs=(placed,) * 4, check_vma=False
    )
```
